128 devices in a mesh: gx: 32 (over x, y, core), gy: 4 (over z).
Axes of the slice: x: 4, y: 4, z: 4, core: 2. Of those that a mesh axis runs over, the one named last changes fastest.
Arguments:
- tokens: bfloat16 [16384, 2048], P(('gx', 'gy')), may hold values from -6 to 6
- expert_ids: int32 [16384, 8], P(('gx', 'gy')), may hold values from 0 to 127, all different within a row; in each aligned block of 128 rows (0 to 127, 128 to 255, ...) at most 24 rows name the same one
- w_gate: bfloat16 [128, 2048, 768], P(('gx', 'gy')), may hold values from -0.125 to 0.125
- w_up: bfloat16 [128, 2048, 768], P(('gx', 'gy')), may hold values from -0.125 to 0.125
- down_error: float32 [128, 768, 2048], P(('gx', 'gy')), may hold values from -18 to 18
Outputs:
- gram_error: float32 [128, 768, 2048], P(('gx', 'gy'))
The draws below stay inside these ranges and needn't reach their ends.
Inputs may be any that keep to these rules, and one draw needn't show every extreme that they name: `expert_ids`: among the rows of one device no expert is named more than 24 times, a bound that some block reaches; every expert is named by some row; the 8 ids of a row are distinct.
All inputs are finite; a program needn't handle non-finite values.
Results may differ from the reference program's by a relative error of at most 0.0036.
Values may be sent and summed in bfloat16 or wider, within the bound.
No kernel may reach another device: no remote copies, remote signals or barrier semaphores. Data moves between devices by JAX's collectives and lax.ppermute only.
A program may use at most 128 MiB of HBM per device.

```python
import math
import jax
import jax.numpy as jnp
import numpy as np
from jax import lax

D = 2048
FF = 768
TOP = 8
TOK_DEV = 128
EXPERTS = 128
TOKENS = 16384
CAP = 24


def shard_levels(stream_key, dims, pieces, low, top_value):
    def one(position, blocks):
        heights = jax.random.uniform(jax.random.fold_in(jax.random.fold_in(stream_key, 6), position), (blocks,), jnp.float32, low / len(pieces), top_value / len(pieces))
        return jnp.repeat(jnp.exp(heights), dims[position] // blocks).reshape((-1,) + (1,) * (len(dims) - position - 1))

    factor_of = one(*pieces[0])
    for cut in pieces[1:]:
        factor_of = factor_of * one(*cut)
    return factor_of


def shared_out(own_key, own, number, rows, count, top, limit, skew):
    sequence = jax.random.permutation(own_key, count)
    packed, ordinary = portions_of(count, rows * top, limit, skew, True), portions_of(count, rows * top, limit, skew, False)
    places = jnp.arange(count)

    def named(sizes, offset_by):
        used = int((sizes > 0).sum())
        fixed = max(1, used // 4)
        shifted = fixed + (places - fixed + offset_by * (used - fixed)) % max(1, count - fixed)
        return jnp.zeros((count,), jnp.int32).at[sequence[jnp.where(places < fixed, places, shifted)]].set(jnp.asarray(sizes, jnp.int32))

    sizes = jnp.where(number % 4 == 0, named(packed, number // 4), named(ordinary, number - number // 4 - 1))
    mixed = jax.random.permutation(jax.random.fold_in(own, 3), count)
    source_of, sink = mixed[0:count // 2 * 2:2], mixed[1:count // 2 * 2:2]
    room = jnp.minimum(sizes[source_of] - 1, limit - sizes[sink]) // 2
    room = jnp.where((source_of == sequence[0]) | (sink == sequence[0]) | (sizes[sink] == 0), 0, jnp.maximum(room, 0))
    shifted = jax.random.randint(jax.random.fold_in(own, 4), (count // 2,), 0, 1 << 20) % (room + 1)
    sizes = sizes.at[source_of].add(-shifted).at[sink].add(shifted)
    items = jnp.searchsorted(jnp.cumsum(sizes), jnp.arange(rows * top), side="right").astype(jnp.int32)
    table = items.reshape(top, rows).T
    table = table[jax.random.permutation(jax.random.fold_in(own, 1), rows)]
    offset_by = jax.random.randint(jax.random.fold_in(own, 2), (rows, 1), 0, top)
    return jnp.take_along_axis(table, (jnp.arange(top)[None, :] + offset_by) % top, axis=1)


def portions_of(number_of, total, limit, lean, full):
    weights = [(1 << 20) // math.isqrt(grade ** lean) + 1 for grade in range(1, number_of + 1)]
    largest = limit if full else min(limit, max(-(-total // number_of), total * weights[0] // sum(weights)))
    least = 1 if total - largest >= number_of - 1 else 0
    holding, rest = [largest] + [least] * (number_of - 1), total - largest - least * (number_of - 1)
    while rest > 0:
        movable = [i for i in range(1, number_of) if holding[i] < largest] or [i for i in range(1, number_of) if holding[i] < limit]
        mass, remaining = sum([weights[i] for i in movable]), rest
        for i in movable:
            extra = min(limit - holding[i], max(1, remaining * weights[i] // mass), rest)
            holding[i] = holding[i] + extra
            rest = rest - extra
    return np.array(holding)


def normal_values(stream_key, shape, scale, bound, shards=(), kind=jnp.bfloat16):
    factor_of = shard_levels(stream_key, shape, shards, -0.22, 0.18) if shards else 1.0
    drawn = jax.random.normal(stream_key, shape, jnp.float32) * scale * factor_of
    return jnp.minimum(jnp.maximum(drawn, -bound), bound).astype(kind)


def setup_inputs(seed: int = 0) -> dict:
    splits = jax.random.split(jax.random.key(seed), 6)
    tokens = normal_values(splits[0], (TOKENS, D), 1.0, 6.0, ((0, 128),))
    expert_ids_keys = jax.random.split(jax.random.fold_in(splits[1], 1), TOKENS // TOK_DEV)
    expert_ids_turns = jax.random.permutation(jax.random.fold_in(splits[1], 3), TOKENS // TOK_DEV)
    expert_ids = jax.vmap(lambda own, number: shared_out(jax.random.fold_in(splits[1], 2), own, number, TOK_DEV, EXPERTS, TOP, CAP, 2))(expert_ids_keys, expert_ids_turns).reshape((TOKENS, TOP))
    w_gate = normal_values(splits[2], (EXPERTS, D, FF), D ** -0.5, 0.125, ((0, 128),))
    w_up = normal_values(splits[3], (EXPERTS, D, FF), D ** -0.5, 0.125, ((0, 128),))
    down_error = normal_values(splits[4], (EXPERTS, FF, D), 3.0, 18.0, ((0, 128),), jnp.float32)
    return dict(tokens=tokens, expert_ids=expert_ids, w_gate=w_gate, w_up=w_up, down_error=down_error)


def reference(tokens, expert_ids, w_gate, w_up, down_error):
    flat_ids = expert_ids.reshape(-1).astype(jnp.int32)
    total = flat_ids.shape[0]
    block_rows = 256
    ordering = jnp.argsort(flat_ids, stable=True).astype(jnp.int32)
    padded_order = jnp.concatenate([ordering, jnp.zeros((block_rows,), jnp.int32)])
    counts = jnp.sum((flat_ids[:, None] == jnp.arange(EXPERTS, dtype=jnp.int32)[None, :]).astype(jnp.int32), axis=0)
    starts = (jnp.cumsum(counts) - counts).astype(jnp.int32)

    def one_expert(expert):
        start = starts[expert]
        count = counts[expert]
        gate_matrix = w_gate[expert]
        up_matrix = w_up[expert]

        def add_block(number, accum):
            offset = (number * block_rows).astype(jnp.int32)
            window = lax.dynamic_slice(padded_order, (start + offset,), (block_rows,))
            live = (offset + jnp.arange(block_rows, dtype=jnp.int32)) < count
            picked = tokens[window // TOP]
            gate = jnp.dot(picked, gate_matrix, preferred_element_type=jnp.float32)
            upward = jnp.dot(picked, up_matrix, preferred_element_type=jnp.float32)
            hidden = jnp.where(live[:, None], jax.nn.silu(gate) * upward, jnp.zeros_like(gate)).astype(jnp.bfloat16)
            return accum + jnp.dot(hidden.T, hidden, preferred_element_type=jnp.float32)

        blocks = ((count + block_rows - 1) // block_rows).astype(jnp.int32)
        gram = lax.fori_loop(jnp.int32(0), blocks, add_block, jnp.zeros((FF, FF), jnp.float32))
        mean_gram = gram / count.astype(jnp.float32)
        return jnp.dot(mean_gram, down_error[expert], preferred_element_type=jnp.float32, precision=lax.Precision.HIGHEST)

    return lax.map(one_expert, jnp.arange(EXPERTS, dtype=jnp.int32))
```

```python
import functools

import jax
import jax.numpy as jnp
from jax import lax
from jax.experimental import pallas as pl
from jax.experimental.pallas import tpu as pltpu
from jax.sharding import PartitionSpec as P

AXES = ("gx", "gy")
FREE = 64.0
LIMIT = 32.0
GROUP = 16
COLS = 512


def pack_kernel(lo, slots, ids_ref, tok_ref, out_ref):
    tokens = tok_ref.shape[0]
    first = pl.program_id(0) * GROUP
    experts = first + lax.broadcasted_iota(jnp.int32, (GROUP, tokens), 0)
    member = jnp.zeros((GROUP, tokens), jnp.float32)
    for k in range(ids_ref.shape[0]):
        member += (ids_ref[k : k + 1, :] == experts).astype(jnp.float32)
    before = (
        lax.broadcasted_iota(jnp.int32, (tokens, tokens), 0)
        < lax.broadcasted_iota(jnp.int32, (tokens, tokens), 1)
    ).astype(jnp.bfloat16)
    rank = jnp.dot(member.astype(jnp.bfloat16), before, preferred_element_type=jnp.float32)
    rank = jnp.where(member > 0.5, rank, -1.0)
    total = jnp.sum(member, axis=1, keepdims=True)
    slot = lo + lax.broadcasted_iota(jnp.int32, (GROUP, slots, tokens), 1)
    slot = slot.astype(jnp.float32)
    picks = (rank[:, None, :] == slot).astype(jnp.float32)
    picks = picks.reshape(GROUP * slots, tokens).astype(jnp.bfloat16)
    rows = jnp.dot(picks, tok_ref[...], preferred_element_type=jnp.float32)
    slot = lo + lax.broadcasted_iota(jnp.int32, (GROUP, slots, 128), 1)
    lane = lax.broadcasted_iota(jnp.int32, (GROUP, slots, 128), 2)
    free = (slot.astype(jnp.float32) >= total[:, :, None]) & (lane == 0)
    mark = jnp.where(free, FREE, 0.0).reshape(GROUP * slots, 128)
    out_ref[:, :128] = (rows[:, :128] + mark).astype(jnp.bfloat16)
    out_ref[:, 128:] = rows[:, 128:].astype(jnp.bfloat16)


def pack(ids_t, tokens, experts, lo, slots):
    top, count = ids_t.shape
    width = tokens.shape[1]
    return pl.pallas_call(
        functools.partial(pack_kernel, lo, slots),
        out_shape=jax.ShapeDtypeStruct((experts * slots, width), jnp.bfloat16),
        grid=(experts // GROUP,),
        in_specs=[
            pl.BlockSpec((top, count), lambda i: (0, 0)),
            pl.BlockSpec((count, width), lambda i: (0, 0)),
        ],
        out_specs=pl.BlockSpec((GROUP * slots, width), lambda i: (i, 0)),
        compiler_params=pltpu.CompilerParams(vmem_limit_bytes=32 << 20),
        cost_estimate=pl.CostEstimate(
            flops=2 * experts * slots * count * width,
            transcendentals=0,
            bytes_accessed=2 * experts * slots * width + 2 * count * width,
        ),
        name="pack_rows",
    )(ids_t, tokens)


def add_tile(x_ref, wg_ref, wu_ref, gram_ref, count_ref):
    x = x_ref[...]
    gate = jnp.dot(x, wg_ref[0], preferred_element_type=jnp.float32)
    upward = jnp.dot(x, wu_ref[0], preferred_element_type=jnp.float32)
    live = x[:, :1].astype(jnp.float32) < LIMIT
    hidden = gate / (1.0 + jnp.exp(-gate)) * upward
    hidden = jnp.where(live, hidden, 0.0).astype(jnp.bfloat16)
    gram_ref[...] += lax.dot_general(
        hidden, hidden, (((0,), (0,)), ((), ())), preferred_element_type=jnp.float32
    )
    count_ref[...] += jnp.sum(live.astype(jnp.float32), axis=0, keepdims=True)


def split(v):
    high = v.astype(jnp.bfloat16)
    return high, (v - high.astype(jnp.float32)).astype(jnp.bfloat16)


def finish_kernel(tiles, x_ref, wg_ref, wu_ref, down_ref, out_ref, gram_ref, count_ref, hi_ref, lo_ref):
    step = pl.program_id(0)

    @pl.when(step == 0)
    def _():
        gram_ref[...] = jnp.zeros_like(gram_ref)
        count_ref[...] = jnp.zeros_like(count_ref)

    @pl.when(step < tiles)
    def _():
        add_tile(x_ref, wg_ref, wu_ref, gram_ref, count_ref)

    @pl.when(step == tiles - 1)
    def _():
        hi_ref[...], lo_ref[...] = split(gram_ref[...] / count_ref[...])

    @pl.when(step >= tiles)
    def _():
        high, low = split(down_ref[0])
        gram_high = hi_ref[...]
        dot = functools.partial(jnp.dot, preferred_element_type=jnp.float32)
        out_ref[0] = dot(gram_high, low) + dot(lo_ref[...], high) + dot(gram_high, high)


def finish(rows, w_gate, w_up, down, tile):
    total, width = rows.shape
    ff = w_gate.shape[2]
    wide = down.shape[2]
    tiles = total // tile
    steps = wide // COLS
    return pl.pallas_call(
        functools.partial(finish_kernel, tiles),
        out_shape=jax.ShapeDtypeStruct(down.shape, jnp.float32),
        grid=(tiles + steps,),
        in_specs=[
            pl.BlockSpec((tile, width), lambda i: (jnp.minimum(i, tiles - 1), 0)),
            pl.BlockSpec((1, width, ff), lambda i: (0, 0, 0)),
            pl.BlockSpec((1, width, ff), lambda i: (0, 0, 0)),
            pl.BlockSpec((1, ff, COLS), lambda i: (0, 0, jnp.maximum(i - tiles, 0))),
        ],
        out_specs=pl.BlockSpec((1, ff, COLS), lambda i: (0, 0, jnp.maximum(i - tiles, 0))),
        scratch_shapes=[
            pltpu.VMEM((ff, ff), jnp.float32),
            pltpu.VMEM((1, 1), jnp.float32),
            pltpu.VMEM((ff, ff), jnp.bfloat16),
            pltpu.VMEM((ff, ff), jnp.bfloat16),
        ],
        compiler_params=pltpu.CompilerParams(vmem_limit_bytes=56 << 20),
        name="hidden_gram_product",
    )(rows, w_gate, w_up, down)


def local(tokens, expert_ids, w_gate, w_up, down_error):
    experts = lax.axis_size("gx") * lax.axis_size("gy")
    count, top = expert_ids.shape
    width = tokens.shape[1]
    slots = 3 * count * top // experts
    ids_t = expert_ids.T
    outgoing = pack(ids_t, tokens, experts, 0, slots).reshape(experts, slots, width)
    received = lax.all_to_all(outgoing, AXES, split_axis=0, concat_axis=0, tiled=True)
    rows = received.reshape(experts * slots, width)
    return finish(rows, w_gate, w_up, down_error, 512)


def solution(mesh):
    return jax.shard_map(
        local,
        mesh=mesh,
        in_specs=(
            P(AXES, None),
            P(AXES, None),
            P(AXES, None, None),
            P(AXES, None, None),
            P(AXES, None, None),
        ),
        out_specs=P(AXES, None, None),
        check_vma=False,
    )
```

```python
import functools
import itertools

import jax
import jax.numpy as jnp
from jax import lax
from jax.experimental import pallas as pl
from jax.experimental.pallas import tpu as pltpu
from jax.sharding import PartitionSpec as P

AXES = ("gx", "gy")
FREE = 64.0
LIMIT = 32.0
RING = 4
SENT = [(shift, cross) for shift in range(RING) for cross in range(2)]
COLS = 512


def place(x, y, c, z):
    return ((x % RING * RING + y % RING) * 2 + c) * RING + z % RING


def routes(target):
    spots = itertools.product(range(RING), range(RING), range(2), range(RING))
    return [(place(*spot), place(*target(*spot))) for spot in spots]


def along_y(shift):
    return routes(lambda x, y, c, z: (x, y + shift, c, z))


def gather_ring(shift):
    return routes(lambda x, y, c, z: (x, y, c, z + shift) if c else (x + shift, y, c, z))


def owner_ring(shift, cross):
    return routes(
        lambda x, y, c, z: (x + shift, y, c ^ cross, z) if c else (x, y, c ^ cross, z + shift)
    )


def move(value, route):
    return lax.ppermute(value, AXES, route)


def pack_kernel(slots, blocks, experts_ref, *refs):
    ins, outs = refs[: len(refs) - len(SENT)], refs[len(refs) - len(SENT) :]
    tokens = ins[0].shape[1]
    width = outs[0].shape[1]
    group = len(SENT)
    top = experts_ref.shape[0]
    experts = experts_ref[...].astype(jnp.float32)
    before = (
        lax.broadcasted_iota(jnp.int32, (tokens, tokens), 0)
        < lax.broadcasted_iota(jnp.int32, (tokens, tokens), 1)
    ).astype(jnp.bfloat16)
    slot = lax.broadcasted_iota(jnp.int32, (group, slots, tokens), 1).astype(jnp.float32)
    lane = lax.broadcasted_iota(jnp.int32, (group, slots, tokens), 2)
    at = 0
    for ref in ins:
        for b in range(ref.shape[0]):
            ids = ref[b, :top, width:].astype(jnp.float32)
            member = jnp.zeros((group, tokens), jnp.float32)
            for k in range(top):
                member += (ids[k : k + 1, :] == experts).astype(jnp.float32)
            rank = jnp.dot(member.astype(jnp.bfloat16), before, preferred_element_type=jnp.float32)
            rank = jnp.where(member > 0.5, rank, -1.0)
            total = jnp.sum(member, axis=1, keepdims=True)
            picks = (rank[:, None, :] == slot).astype(jnp.float32)
            picks = picks.reshape(group * slots, tokens).astype(jnp.bfloat16)
            rows = jnp.dot(picks, ref[b, :, :width], preferred_element_type=jnp.float32)
            free = (slot >= total[:, :, None]) & (lane == 0)
            mark = jnp.where(free, FREE, 0.0).reshape(group * slots, tokens)
            for g, out in enumerate(outs):
                here = slice(g * slots, (g + 1) * slots)
                spot = slice(at * slots, (at + 1) * slots)
                out[spot, :tokens] = (rows[here, :tokens] + mark[here]).astype(jnp.bfloat16)
                out[spot, tokens:] = rows[here, tokens:].astype(jnp.bfloat16)
            at += 1


def pack(slots, width, experts, parts):
    blocks = sum(part.shape[0] for part in parts)
    shape = jax.ShapeDtypeStruct((blocks * slots, width), jnp.bfloat16)
    tokens = parts[0].shape[1]
    rows = len(SENT) * blocks * slots
    return pl.pallas_call(
        functools.partial(pack_kernel, slots, blocks),
        out_shape=[shape] * len(SENT),
        in_specs=[pl.BlockSpec(memory_space=pltpu.VMEM)] * (1 + len(parts)),
        out_specs=[pl.BlockSpec(memory_space=pltpu.VMEM)] * len(SENT),
        compiler_params=pltpu.CompilerParams(vmem_limit_bytes=40 << 20),
        cost_estimate=pl.CostEstimate(
            flops=2 * rows * tokens * width,
            transcendentals=0,
            bytes_accessed=2 * rows * width + 2 * blocks * tokens * width,
        ),
        name="pack_rows",
    )(experts, *parts)


def split(v):
    high = v.astype(jnp.bfloat16)
    return high, (v - high.astype(jnp.float32)).astype(jnp.bfloat16)


def consume_kernel(more, last, *refs):
    parts = len(SENT)
    rows, refs = refs[:parts], refs[parts:]
    (wg_hbm, wu_hbm), refs = refs[:2], refs[2:]
    if more:
        (gram_hbm, count_in), refs = refs[:2], refs[2:]
    if last:
        down_hbm, out_hbm, refs = refs[0], refs[1], refs[2:]
        out_sem, refs = refs[0], refs[1:]
        down, out, high_ref, low_ref, refs = *refs[:4], refs[4:]
        gram_ref, refs = refs[0], refs[1:]
    else:
        (gram_ref, count_ref), refs = refs[:2], refs[2:]
    sem, x, wg, wu, h = refs[:5]
    n = rows[0].shape[0]
    copies = [pltpu.make_async_copy(rows[j], x.at[pl.ds(j * n, n)], sem.at[j]) for j in range(parts)]
    get_wg = pltpu.make_async_copy(wg_hbm.at[0], wg, sem.at[parts])
    get_wu = pltpu.make_async_copy(wu_hbm.at[0], wu, sem.at[parts + 1])
    copies[0].start()
    copies[1].start()
    get_wg.start()
    get_wu.start()
    for copy in copies[2:]:
        copy.start()
    if more:
        get_gram = pltpu.make_async_copy(gram_hbm, gram_ref, sem.at[parts + 2])
        get_gram.start()
    if last:
        get_down = pltpu.make_async_copy(down_hbm.at[0], down, sem.at[parts + 3])
        get_down.start()
    count = count_in[...] if more else jnp.zeros((1, 1), jnp.float32)
    for j in range(0, parts, 2):
        copies[j].wait()
        copies[j + 1].wait()
        if j == 0:
            get_wg.wait()
        tile = x[pl.ds(j * n, 2 * n), :]
        gate = jnp.dot(tile, wg[...], preferred_element_type=jnp.float32)
        if j == 0:
            get_wu.wait()
        upward = jnp.dot(tile, wu[...], preferred_element_type=jnp.float32)
        live = tile[:, :1].astype(jnp.float32) < LIMIT
        hidden = gate / (1.0 + jnp.exp(-gate)) * upward
        h[pl.ds(j * n, 2 * n), :] = jnp.where(live, hidden, 0.0).astype(jnp.bfloat16)
        count += jnp.sum(live.astype(jnp.float32), axis=0, keepdims=True)
    gram = lax.dot_general(
        h[...], h[...], (((0,), (0,)), ((), ())), preferred_element_type=jnp.float32
    )
    if more:
        get_gram.wait()
        gram += gram_ref[...]
    if not last:
        gram_ref[...] = gram
        count_ref[...] = count
        return
    high_ref[...], low_ref[...] = split(gram / count)
    get_down.wait()
    dot = functools.partial(jnp.dot, preferred_element_type=jnp.float32)
    puts = []
    for k in range(down.shape[1] // COLS):
        cols = pl.ds(k * COLS, COLS)
        high, low = split(down[:, cols])
        gram_high = high_ref[...]
        out[:, cols] = dot(gram_high, low) + dot(low_ref[...], high) + dot(gram_high, high)
        put = pltpu.make_async_copy(out.at[:, cols], out_hbm.at[0, :, cols], out_sem.at[k])
        put.start()
        puts.append(put)
    for put in puts:
        put.wait()


def consume(rows, w_gate, w_up, before=(), down=None):
    n, width = rows[0].shape
    ff = w_gate.shape[2]
    total = n * len(rows)
    more, last = bool(before), down is not None
    hbm, vmem = pl.BlockSpec(memory_space=pl.ANY), pl.BlockSpec(memory_space=pltpu.VMEM)
    operands = [*rows, w_gate, w_up]
    specs = [hbm] * len(operands)
    if more:
        operands += before
        specs += [hbm, vmem]
    scratch = []
    flops = 4 * total * width * ff + 2 * total * ff * ff
    if last:
        wide = down.shape[2]
        operands.append(down)
        specs.append(hbm)
        out_shape, out_specs = jax.ShapeDtypeStruct(down.shape, jnp.float32), hbm
        scratch = [
            pltpu.SemaphoreType.DMA((wide // COLS,)),
            pltpu.VMEM((ff, wide), jnp.float32),
            pltpu.VMEM((ff, wide), jnp.float32),
            pltpu.VMEM((ff, ff), jnp.bfloat16),
            pltpu.VMEM((ff, ff), jnp.bfloat16),
            pltpu.VMEM((ff, ff), jnp.float32),
        ]
        flops += 6 * ff * ff * wide
    else:
        out_shape = [
            jax.ShapeDtypeStruct((ff, ff), jnp.float32),
            jax.ShapeDtypeStruct((1, 1), jnp.float32),
        ]
        out_specs = [vmem, vmem]
    scratch += [
        pltpu.SemaphoreType.DMA((len(rows) + 4,)),
        pltpu.VMEM((total, width), jnp.bfloat16),
        pltpu.VMEM((width, ff), jnp.bfloat16),
        pltpu.VMEM((width, ff), jnp.bfloat16),
        pltpu.VMEM((total, ff), jnp.bfloat16),
    ]
    return pl.pallas_call(
        functools.partial(consume_kernel, more, last),
        out_shape=out_shape,
        in_specs=specs,
        out_specs=out_specs,
        scratch_shapes=scratch,
        compiler_params=pltpu.CompilerParams(vmem_limit_bytes=56 << 20),
        cost_estimate=pl.CostEstimate(
            flops=flops,
            transcendentals=total * ff,
            bytes_accessed=2 * total * width + 4 * width * ff,
        ),
        name="hidden_gram",
    )(*operands)


def exchange(packed):
    order = [2, 1, 3, 0]
    out = [None] * len(SENT)
    for cross in range(2):
        for shift in order:
            at = SENT.index((shift, cross))
            if shift or cross:
                out[at] = move(packed[at], owner_ring(shift, cross))
            else:
                out[at] = packed[at]
    return out


def local(tokens, expert_ids, w_gate, w_up, down_error):
    experts = lax.axis_size("gx") * lax.axis_size("gy")
    count, top = expert_ids.shape
    width = tokens.shape[1]
    slots = 3 * count * top // experts
    wide, deep = lax.axis_index("gx"), lax.axis_index("gy")
    core, column, line = wide % 2, wide // 2 % RING, wide // (2 * RING)
    targets = []
    for shift, cross in SENT:
        other = core ^ cross
        on_z = ((line * RING + column) * 2 + other) * RING + (deep + shift) % RING
        on_x = (((line + shift) % RING * RING + column) * 2 + other) * RING + deep
        targets.append(jnp.where(core == 0, on_z, on_x))
    targets = jnp.broadcast_to(jnp.stack(targets).astype(jnp.int32)[:, None], (len(SENT), count))
    ids = jnp.pad(expert_ids.T.astype(jnp.bfloat16), ((0, count - top), (0, 0)))
    own = jnp.concatenate([tokens, ids], axis=1)[None]

    ring = [move(own, gather_ring(shift)) for shift in (2, 1, -1)]
    own_up, own_down = move(own, along_y(1)), move(own, along_y(-1))
    rest = jnp.concatenate(ring, axis=0)
    rest_up, rest_down = move(rest, along_y(1)), move(rest, along_y(-1))
    far = [
        move(own_up, along_y(1)),
        move(rest_up[:1], along_y(1)),
        move(rest_down[1:], along_y(-1)),
    ]
    first = exchange(pack(slots, width, targets, [own, *ring, own_up, own_down]))
    second = exchange(pack(slots, width, targets, [rest_up, rest_down]))
    third = exchange(pack(slots, width, targets, far))
    sums = consume(first, w_gate, w_up)
    sums = consume(second, w_gate, w_up, sums)
    return consume(third, w_gate, w_up, sums, down_error)


def solution(mesh):
    return jax.shard_map(
        local,
        mesh=mesh,
        in_specs=(
            P(AXES, None),
            P(AXES, None),
            P(AXES, None, None),
            P(AXES, None, None),
            P(AXES, None, None),
        ),
        out_specs=P(AXES, None, None),
        check_vma=False,
    )
```

```python
import functools
import itertools

import jax
import jax.numpy as jnp
import numpy as np
from jax import lax
from jax.experimental import pallas as pl
from jax.experimental.pallas import tpu as pltpu
from jax.sharding import PartitionSpec as P

AXES = ("gx", "gy")
FREE = 64.0
LIMIT = 32.0
RING = 4
EXTRA = 8
SENT = [(shift, cross) for shift in range(RING) for cross in range(2)]
COLS = 512


def place(x, y, c, z):
    return ((x % RING * RING + y % RING) * 2 + c) * RING + z % RING


SPOTS = list(itertools.product(range(RING), range(RING), range(2), range(RING)))


def owner(shift, cross, x, y, c, z):
    return place(x + shift, y, c ^ cross, z) if c else place(x, y, c ^ cross, z + shift)


TARGETS = np.array([[owner(*sent, *spot) for sent in SENT] for spot in SPOTS], np.int32)


def along_y(shift):
    return [(place(x, y, c, z), place(x, y + shift, c, z)) for x, y, c, z in SPOTS]


def gather_ring(shift):
    return [
        (place(x, y, c, z), place(x, y, c, z + shift) if c else place(x + shift, y, c, z))
        for x, y, c, z in SPOTS
    ]


def owner_ring(shift):
    return [(place(*spot), owner(shift, 0, *spot)) for spot in SPOTS]


OTHER_CORE = [(place(x, y, c, z), place(x, y, 1 - c, z)) for x, y, c, z in SPOTS]


def move(value, route, name="y"):
    with jax.named_scope(name):
        return lax.ppermute(value, AXES, route)


def tie(*values):
    return lax.optimization_barrier(values)


def pack_kernel(slots, experts_ref, *refs):
    ins, outs = refs[:-RING], refs[-RING:]
    tokens = ins[0].shape[1]
    width = outs[0].shape[2]
    group = len(SENT)
    top = experts_ref.shape[0]
    experts = experts_ref[...].astype(jnp.float32)
    before = (
        lax.broadcasted_iota(jnp.int32, (tokens, tokens), 0)
        < lax.broadcasted_iota(jnp.int32, (tokens, tokens), 1)
    ).astype(jnp.bfloat16)
    slot = lax.broadcasted_iota(jnp.int32, (group, slots, tokens), 1).astype(jnp.float32)
    lane = lax.broadcasted_iota(jnp.int32, (group, slots, tokens), 2)
    at = 0
    for ref in ins:
        for b in range(ref.shape[0]):
            ids = ref[b, :top, width:].astype(jnp.float32)
            member = jnp.zeros((group, tokens), jnp.float32)
            for k in range(top):
                member += (ids[k : k + 1, :] == experts).astype(jnp.float32)
            rank = jnp.dot(member.astype(jnp.bfloat16), before, preferred_element_type=jnp.float32)
            rank = jnp.where(member > 0.5, rank, -1.0)
            total = jnp.sum(member, axis=1, keepdims=True)
            picks = (rank[:, None, :] == slot).astype(jnp.float32)
            picks = picks.reshape(group * slots, tokens).astype(jnp.bfloat16)
            rows = jnp.dot(picks, ref[b, :, :width], preferred_element_type=jnp.float32)
            free = (slot >= total[:, :, None]) & (lane == 0)
            mark = jnp.where(free, FREE, 0.0).reshape(group * slots, tokens)
            for g, (shift, cross) in enumerate(SENT):
                here = slice(g * slots, (g + 1) * slots)
                spot = slice(at * slots, (at + 1) * slots)
                out = outs[shift]
                out[cross, spot, :tokens] = (rows[here, :tokens] + mark[here]).astype(jnp.bfloat16)
                out[cross, spot, tokens:] = rows[here, tokens:].astype(jnp.bfloat16)
            at += 1


def pack(slots, width, experts, parts):
    blocks = sum(part.shape[0] for part in parts)
    shape = jax.ShapeDtypeStruct((2, blocks * slots, width), jnp.bfloat16)
    tokens = parts[0].shape[1]
    rows = len(SENT) * blocks * slots
    return pl.pallas_call(
        functools.partial(pack_kernel, slots),
        out_shape=[shape] * RING,
        in_specs=[pl.BlockSpec(memory_space=pltpu.VMEM)] * (1 + len(parts)),
        out_specs=[pl.BlockSpec(memory_space=pltpu.VMEM)] * RING,
        compiler_params=pltpu.CompilerParams(vmem_limit_bytes=24 << 20),
        cost_estimate=pl.CostEstimate(
            flops=2 * rows * tokens * width,
            transcendentals=0,
            bytes_accessed=2 * rows * width + 2 * blocks * tokens * width,
        ),
        name="pack_rows",
    )(experts, *parts)


def consume_kernel(which, more, *refs):
    rows, (wg, wu), refs = refs[:RING], refs[RING : RING + 2], refs[RING + 2 :]
    if more:
        before_ref, refs = refs[0], refs[1:]
    sum_ref, sem, x, h = refs
    n = rows[0].shape[1]
    ff = h.shape[1]
    copies = [
        pltpu.make_async_copy(rows[j].at[which], x.at[pl.ds(j * n, n)], sem.at[j])
        for j in range(RING)
    ]
    for copy in copies:
        copy.start()
    count = before_ref[ff:, :1] if more else jnp.zeros((EXTRA, 1), jnp.float32)
    group = RING if n < 128 else 2
    for j in range(0, RING, group):
        for copy in copies[j : j + group]:
            copy.wait()
        tile = x[pl.ds(j * n, group * n), :]
        gate = jnp.dot(tile, wg[0], preferred_element_type=jnp.float32)
        upward = jnp.dot(tile, wu[0], preferred_element_type=jnp.float32)
        live = tile[:, :1].astype(jnp.float32) < LIMIT
        hidden = gate / (1.0 + jnp.exp(-gate)) * upward
        h[pl.ds(j * n, group * n), :] = jnp.where(live, hidden, 0.0).astype(jnp.bfloat16)
        count += jnp.sum(live.astype(jnp.float32), axis=0, keepdims=True)
    gram = lax.dot_general(
        h[...], h[...], (((0,), (0,)), ((), ())), preferred_element_type=jnp.float32
    )
    sum_ref[:ff, :] = gram + before_ref[:ff, :] if more else gram
    sum_ref[ff:, :] = jnp.broadcast_to(count, (EXTRA, ff))


def consume(which, rows, w_gate, w_up, before=None):
    _, n, width = rows[0].shape
    ff = w_gate.shape[2]
    total = n * RING
    more = before is not None
    hbm, vmem = pl.BlockSpec(memory_space=pl.ANY), pl.BlockSpec(memory_space=pltpu.VMEM)
    operands = [*rows, w_gate, w_up]
    specs = [hbm] * RING + [vmem] * 2
    if more:
        operands.append(before)
        specs.append(vmem)
    return pl.pallas_call(
        functools.partial(consume_kernel, which, more),
        out_shape=jax.ShapeDtypeStruct((ff + EXTRA, ff), jnp.float32),
        in_specs=specs,
        out_specs=vmem,
        scratch_shapes=[
            pltpu.SemaphoreType.DMA((RING,)),
            pltpu.VMEM((total, width), jnp.bfloat16),
            pltpu.VMEM((total, ff), jnp.bfloat16),
        ],
        compiler_params=pltpu.CompilerParams(vmem_limit_bytes=28 << 20),
        cost_estimate=pl.CostEstimate(
            flops=4 * total * width * ff + 2 * total * ff * ff,
            transcendentals=total * ff,
            bytes_accessed=2 * total * width + 4 * width * ff + 8 * ff * ff,
        ),
        name="hidden_gram",
    )(*operands)


def finish_kernel(one_ref, two_ref, down_ref, out_ref, mean_ref):
    ff = mean_ref.shape[0]

    @pl.when(pl.program_id(0) == 0)
    def _():
        count = one_ref[ff : ff + 1, :1] + two_ref[ff : ff + 1, :1]
        mean = (one_ref[:ff, :] + two_ref[:ff, :]) / count
        mean_ref[...] = mean.astype(jnp.bfloat16)

    down = down_ref[0].astype(jnp.bfloat16)
    out_ref[0] = jnp.dot(mean_ref[...], down, preferred_element_type=jnp.float32)


def finish(one, two, down):
    _, ff, wide = down.shape
    part = pl.BlockSpec((1, ff, COLS), lambda i: (0, 0, i))
    whole = pl.BlockSpec(one.shape, lambda i: (0, 0))
    return pl.pallas_call(
        finish_kernel,
        out_shape=jax.ShapeDtypeStruct(down.shape, jnp.float32),
        grid=(wide // COLS,),
        in_specs=[whole, whole, part],
        out_specs=part,
        scratch_shapes=[pltpu.VMEM((ff, ff), jnp.bfloat16)],
        compiler_params=pltpu.CompilerParams(vmem_limit_bytes=28 << 20),
        name="mean_product",
    )(one, two, down)


def exchange(packed):
    sent = [move(packed[shift], owner_ring(shift), "F") for shift in (2, 1, 3)]
    return [packed[0], *sent]


def local(tokens, expert_ids, w_gate, w_up, down_error):
    experts = lax.axis_size("gx") * lax.axis_size("gy")
    count, top = expert_ids.shape
    width = tokens.shape[1]
    slots = 3 * count * top // experts
    me = lax.axis_index(AXES)
    targets = lax.dynamic_slice(jnp.asarray(TARGETS), (me, 0), (1, len(SENT)))
    targets = jnp.broadcast_to(targets[0][:, None], (len(SENT), count))
    ids = jnp.pad(expert_ids.T.astype(jnp.bfloat16), ((0, count - top), (0, 0)))
    own = jnp.concatenate([tokens, ids], axis=1)[None]

    def packed(*parts):
        return pack(slots, width, targets, parts)

    ring = [move(own, gather_ring(shift), "ring") for shift in (2, 1, -1)]
    own_up, own_down = move(own, along_y(1), "own"), move(own, along_y(-1), "own")
    *ring, own_up, own_down = tie(*ring, own_up, own_down)
    near = jnp.concatenate(ring, axis=0)
    near, own = tie(near, own)
    near_up, near_down = move(near, along_y(1), "near"), move(near, along_y(-1), "near")
    rows_a = exchange(packed(own, *ring, own_up, own_down))
    mine = consume(0, rows_a, w_gate, w_up)
    near_up, near_down, mine, other_gate, other_up, *rows_a = tie(
        near_up, near_down, mine, w_gate, w_up, *rows_a
    )
    other_gate, other_up = move(other_gate, OTHER_CORE, "og"), move(other_up, OTHER_CORE, "ou")
    next_up = jnp.concatenate([own_up, near_up[:1]], axis=0)
    far_up, far_down = move(next_up, along_y(1), "far"), move(near_down[1:], along_y(-1), "far")
    rows_b = exchange(packed(near_up, near_down))
    theirs = consume(1, rows_a, other_gate, other_up)
    far_up, far_down, theirs, *rows_b = tie(far_up, far_down, theirs, *rows_b)
    rows_c = exchange(packed(far_up, far_down))
    mine = consume(0, rows_b, w_gate, w_up, mine)
    theirs = consume(1, rows_b, other_gate, other_up, theirs)
    mine, theirs, *rows_c = tie(mine, theirs, *rows_c)
    theirs = move(consume(1, rows_c, other_gate, other_up, theirs), OTHER_CORE, "sums")
    mine = consume(0, rows_c, w_gate, w_up, mine)
    return finish(mine, theirs, down_error)


def solution(mesh):
    return jax.shard_map(
        local,
        mesh=mesh,
        in_specs=(
            P(AXES, None),
            P(AXES, None),
            P(AXES, None, None),
            P(AXES, None, None),
            P(AXES, None, None),
        ),
        out_specs=P(AXES, None, None),
        check_vma=False,
    )
```

```python
import functools
import itertools

import jax
import jax.numpy as jnp
import numpy as np
from jax import lax
from jax.experimental import pallas as pl
from jax.experimental.pallas import tpu as pltpu
from jax.sharding import PartitionSpec as P

AXES = ("gx", "gy")
FREE = 64.0
LIMIT = 32.0
RING = 4
EXTRA = 8
SENT = [(shift, cross) for shift in range(RING) for cross in range(2)]
COLS = 512


def place(x, y, c, z):
    return ((x % RING * RING + y % RING) * 2 + c) * RING + z % RING


SPOTS = list(itertools.product(range(RING), range(RING), range(2), range(RING)))


def owner(shift, cross, x, y, c, z):
    return place(x + shift, y, c ^ cross, z) if c else place(x, y, c ^ cross, z + shift)


TARGETS = np.array([[owner(*sent, *spot) for sent in SENT] for spot in SPOTS], np.int32)


def along_y(shift):
    return [(place(x, y, c, z), place(x, y + shift, c, z)) for x, y, c, z in SPOTS]


def gather_ring(shift):
    return [
        (place(x, y, c, z), place(x, y, c, z + shift) if c else place(x + shift, y, c, z))
        for x, y, c, z in SPOTS
    ]


def owner_ring(shift):
    return [(place(*spot), owner(shift, 0, *spot)) for spot in SPOTS]


OTHER_CORE = [(place(x, y, c, z), place(x, y, 1 - c, z)) for x, y, c, z in SPOTS]


def move(value, route, name="y"):
    with jax.named_scope(name):
        return lax.ppermute(value, AXES, route)


def tie(*values):
    return lax.optimization_barrier(values)


def pack_kernel(slots, experts_ref, *refs):
    ins, outs = refs[:-RING], refs[-RING:]
    tokens = ins[0].shape[1]
    width = outs[0].shape[2]
    group = len(SENT)
    top = experts_ref.shape[0]
    experts = experts_ref[...].astype(jnp.float32)
    before = (
        lax.broadcasted_iota(jnp.int32, (tokens, tokens), 0)
        < lax.broadcasted_iota(jnp.int32, (tokens, tokens), 1)
    ).astype(jnp.bfloat16)
    slot = lax.broadcasted_iota(jnp.int32, (group, slots, tokens), 1).astype(jnp.float32)
    lane = lax.broadcasted_iota(jnp.int32, (group, slots, tokens), 2)
    at = 0
    for ref in ins:
        for b in range(ref.shape[0]):
            ids = ref[b, :top, width:].astype(jnp.float32)
            member = jnp.zeros((group, tokens), jnp.float32)
            for k in range(top):
                member += (ids[k : k + 1, :] == experts).astype(jnp.float32)
            rank = jnp.dot(member.astype(jnp.bfloat16), before, preferred_element_type=jnp.float32)
            rank = jnp.where(member > 0.5, rank, -1.0)
            total = jnp.sum(member, axis=1, keepdims=True)
            picks = (rank[:, None, :] == slot).astype(jnp.float32)
            picks = picks.reshape(group * slots, tokens).astype(jnp.bfloat16)
            rows = jnp.dot(picks, ref[b, :, :width], preferred_element_type=jnp.float32)
            free = (slot >= total[:, :, None]) & (lane == 0)
            mark = jnp.where(free, FREE, 0.0).reshape(group * slots, tokens)
            for g, (shift, cross) in enumerate(SENT):
                here = slice(g * slots, (g + 1) * slots)
                spot = slice(at * slots, (at + 1) * slots)
                out = outs[shift]
                out[cross, spot, :tokens] = (rows[here, :tokens] + mark[here]).astype(jnp.bfloat16)
                out[cross, spot, tokens:] = rows[here, tokens:].astype(jnp.bfloat16)
            at += 1


def pack(slots, width, experts, parts):
    blocks = sum(part.shape[0] for part in parts)
    shape = jax.ShapeDtypeStruct((2, blocks * slots, width), jnp.bfloat16)
    tokens = parts[0].shape[1]
    rows = len(SENT) * blocks * slots
    return pl.pallas_call(
        functools.partial(pack_kernel, slots),
        out_shape=[shape] * RING,
        in_specs=[pl.BlockSpec(memory_space=pltpu.VMEM)] * (1 + len(parts)),
        out_specs=[pl.BlockSpec(memory_space=pltpu.VMEM)] * RING,
        compiler_params=pltpu.CompilerParams(vmem_limit_bytes=24 << 20),
        cost_estimate=pl.CostEstimate(
            flops=2 * rows * tokens * width,
            transcendentals=0,
            bytes_accessed=2 * rows * width + 2 * blocks * tokens * width,
        ),
        name="pack_rows",
    )(experts, *parts)


def consume_kernel(which, more, *refs):
    rows, (wg, wu), refs = refs[:RING], refs[RING : RING + 2], refs[RING + 2 :]
    if more:
        before_ref, refs = refs[0], refs[1:]
    sum_ref, sem, x, h = refs
    n = rows[0].shape[1]
    ff = h.shape[1]
    copies = [
        pltpu.make_async_copy(rows[j].at[which], x.at[pl.ds(j * n, n)], sem.at[j])
        for j in range(RING)
    ]
    for copy in copies:
        copy.start()
    count = before_ref[ff:, :1] if more else jnp.zeros((EXTRA, 1), jnp.float32)
    group = RING if n < 128 else 2
    for j in range(0, RING, group):
        for copy in copies[j : j + group]:
            copy.wait()
        tile = x[pl.ds(j * n, group * n), :]
        gate = jnp.dot(tile, wg[0], preferred_element_type=jnp.float32)
        upward = jnp.dot(tile, wu[0], preferred_element_type=jnp.float32)
        live = tile[:, :1].astype(jnp.float32) < LIMIT
        hidden = gate / (1.0 + jnp.exp(-gate)) * upward
        h[pl.ds(j * n, group * n), :] = jnp.where(live, hidden, 0.0).astype(jnp.bfloat16)
        count += jnp.sum(live.astype(jnp.float32), axis=0, keepdims=True)
    gram = lax.dot_general(
        h[...], h[...], (((0,), (0,)), ((), ())), preferred_element_type=jnp.float32
    )
    sum_ref[:ff, :] = gram + before_ref[:ff, :] if more else gram
    sum_ref[ff:, :] = jnp.broadcast_to(count, (EXTRA, ff))


def consume(which, rows, w_gate, w_up, before=None):
    _, n, width = rows[0].shape
    ff = w_gate.shape[2]
    total = n * RING
    more = before is not None
    hbm, vmem = pl.BlockSpec(memory_space=pl.ANY), pl.BlockSpec(memory_space=pltpu.VMEM)
    operands = [*rows, w_gate, w_up]
    specs = [hbm] * RING + [vmem] * 2
    if more:
        operands.append(before)
        specs.append(vmem)
    return pl.pallas_call(
        functools.partial(consume_kernel, which, more),
        out_shape=jax.ShapeDtypeStruct((ff + EXTRA, ff), jnp.float32),
        in_specs=specs,
        out_specs=vmem,
        scratch_shapes=[
            pltpu.SemaphoreType.DMA((RING,)),
            pltpu.VMEM((total, width), jnp.bfloat16),
            pltpu.VMEM((total, ff), jnp.bfloat16),
        ],
        compiler_params=pltpu.CompilerParams(vmem_limit_bytes=28 << 20),
        cost_estimate=pl.CostEstimate(
            flops=4 * total * width * ff + 2 * total * ff * ff,
            transcendentals=total * ff,
            bytes_accessed=2 * total * width + 4 * width * ff + 8 * ff * ff,
        ),
        name="hidden_gram",
    )(*operands)


def finish_kernel(one_ref, two_ref, down_ref, out_ref, mean_ref):
    ff = mean_ref.shape[0]

    @pl.when(pl.program_id(0) == 0)
    def _():
        count = one_ref[ff : ff + 1, :1] + two_ref[ff : ff + 1, :1]
        mean = (one_ref[:ff, :] + two_ref[:ff, :]) / count
        mean_ref[...] = mean.astype(jnp.bfloat16)

    down = down_ref[0].astype(jnp.bfloat16)
    out_ref[0] = jnp.dot(mean_ref[...], down, preferred_element_type=jnp.float32)


def finish(one, two, down):
    _, ff, wide = down.shape
    part = pl.BlockSpec((1, ff, COLS), lambda i: (0, 0, i))
    whole = pl.BlockSpec(one.shape, lambda i: (0, 0))
    return pl.pallas_call(
        finish_kernel,
        out_shape=jax.ShapeDtypeStruct(down.shape, jnp.float32),
        grid=(wide // COLS,),
        in_specs=[whole, whole, part],
        out_specs=part,
        scratch_shapes=[pltpu.VMEM((ff, ff), jnp.bfloat16)],
        compiler_params=pltpu.CompilerParams(vmem_limit_bytes=28 << 20),
        name="mean_product",
    )(one, two, down)


def exchange(packed):
    sent = [move(packed[shift], owner_ring(shift), "F") for shift in (2, 1, 3)]
    return [packed[0], *sent]


def local(tokens, expert_ids, w_gate, w_up, down_error):
    experts = lax.axis_size("gx") * lax.axis_size("gy")
    count, top = expert_ids.shape
    width = tokens.shape[1]
    slots = 3 * count * top // experts
    me = lax.axis_index(AXES)
    targets = lax.dynamic_slice(jnp.asarray(TARGETS), (me, 0), (1, len(SENT)))
    targets = jnp.broadcast_to(targets[0][:, None], (len(SENT), count))
    ids = jnp.pad(expert_ids.T.astype(jnp.bfloat16), ((0, count - top), (0, 0)))
    own = jnp.concatenate([tokens, ids], axis=1)[None]

    def packed(*parts):
        return pack(slots, width, targets, parts)

    ring = [move(own, gather_ring(shift), "ring") for shift in (2, 1, -1)]
    own_up, own_down = move(own, along_y(1), "own"), move(own, along_y(-1), "own")
    ring = tie(*ring)
    near = jnp.concatenate(ring, axis=0)
    near, own = tie(near, own)
    near_up, near_down = move(near, along_y(1), "near"), move(near, along_y(-1), "near")
    rows_a = exchange(packed(own, *ring, own_up, own_down))
    mine = consume(0, rows_a, w_gate, w_up)
    near_up, near_down, mine, other_gate, other_up, *rows_a = tie(
        near_up, near_down, mine, w_gate, w_up, *rows_a
    )
    other_gate, other_up = move(other_gate, OTHER_CORE, "og"), move(other_up, OTHER_CORE, "ou")
    next_up = jnp.concatenate([own_up, near_up[:1]], axis=0)
    far_up, far_down = move(next_up, along_y(1), "far"), move(near_down[1:], along_y(-1), "far")
    rows_b = exchange(packed(near_up, near_down))
    theirs = consume(1, rows_a, other_gate, other_up)
    far_up, far_down, theirs, *rows_b = tie(far_up, far_down, theirs, *rows_b)
    rows_c = exchange(packed(far_up, far_down))
    mine = consume(0, rows_b, w_gate, w_up, mine)
    theirs = consume(1, rows_b, other_gate, other_up, theirs)
    mine, theirs, *rows_c = tie(mine, theirs, *rows_c)
    theirs = move(consume(1, rows_c, other_gate, other_up, theirs), OTHER_CORE, "sums")
    mine = consume(0, rows_c, w_gate, w_up, mine)
    return finish(mine, theirs, down_error)


def solution(mesh):
    return jax.shard_map(
        local,
        mesh=mesh,
        in_specs=(
            P(AXES, None),
            P(AXES, None),
            P(AXES, None, None),
            P(AXES, None, None),
            P(AXES, None, None),
        ),
        out_specs=P(AXES, None, None),
        check_vma=False,
    )
```

```python
import functools
import itertools

import jax
import jax.numpy as jnp
import numpy as np
from jax import lax
from jax.experimental import pallas as pl
from jax.experimental.pallas import tpu as pltpu
from jax.sharding import PartitionSpec as P

AXES = ("gx", "gy")
FREE = 64.0
LIMIT = 32.0
RING = 4
EXTRA = 8
SENT = [(shift, cross) for shift in range(RING) for cross in range(2)]
COLS = 512


def place(x, y, c, z):
    return ((x % RING * RING + y % RING) * 2 + c) * RING + z % RING


SPOTS = list(itertools.product(range(RING), range(RING), range(2), range(RING)))


def owner(shift, cross, x, y, c, z):
    return place(x + shift, y, c ^ cross, z) if c else place(x, y, c ^ cross, z + shift)


TARGETS = np.array([[owner(*sent, *spot) for sent in SENT] for spot in SPOTS], np.int32)


def along_y(shift):
    return [(place(x, y, c, z), place(x, y + shift, c, z)) for x, y, c, z in SPOTS]


def gather_ring(shift):
    return [
        (place(x, y, c, z), place(x, y, c, z + shift) if c else place(x + shift, y, c, z))
        for x, y, c, z in SPOTS
    ]


def owner_ring(shift):
    return [(place(*spot), owner(shift, 0, *spot)) for spot in SPOTS]


OTHER_CORE = [(place(x, y, c, z), place(x, y, 1 - c, z)) for x, y, c, z in SPOTS]


def move(value, route, name="y"):
    with jax.named_scope(name):
        return lax.ppermute(value, AXES, route)


def tie(*values):
    return lax.optimization_barrier(values)


def pack_kernel(slots, experts_ref, *refs):
    ins, outs = refs[:-RING], refs[-RING:]
    tokens = ins[0].shape[1]
    width = outs[0].shape[2]
    group = len(SENT)
    top = experts_ref.shape[0]
    experts = experts_ref[...].astype(jnp.float32)
    before = (
        lax.broadcasted_iota(jnp.int32, (tokens, tokens), 0)
        < lax.broadcasted_iota(jnp.int32, (tokens, tokens), 1)
    ).astype(jnp.bfloat16)
    slot = lax.broadcasted_iota(jnp.int32, (group, slots, tokens), 1).astype(jnp.float32)
    lane = lax.broadcasted_iota(jnp.int32, (group, slots, tokens), 2)
    at = 0
    for ref in ins:
        for b in range(ref.shape[0]):
            ids = ref[b, :top, width:].astype(jnp.float32)
            member = jnp.zeros((group, tokens), jnp.float32)
            for k in range(top):
                member += (ids[k : k + 1, :] == experts).astype(jnp.float32)
            rank = jnp.dot(member.astype(jnp.bfloat16), before, preferred_element_type=jnp.float32)
            rank = jnp.where(member > 0.5, rank, -1.0)
            total = jnp.sum(member, axis=1, keepdims=True)
            picks = (rank[:, None, :] == slot).astype(jnp.float32)
            picks = picks.reshape(group * slots, tokens).astype(jnp.bfloat16)
            rows = jnp.dot(picks, ref[b, :, :width], preferred_element_type=jnp.float32)
            free = (slot >= total[:, :, None]) & (lane == 0)
            mark = jnp.where(free, FREE, 0.0).reshape(group * slots, tokens)
            for g, (shift, cross) in enumerate(SENT):
                here = slice(g * slots, (g + 1) * slots)
                spot = slice(at * slots, (at + 1) * slots)
                out = outs[shift]
                out[cross, spot, :tokens] = (rows[here, :tokens] + mark[here]).astype(jnp.bfloat16)
                out[cross, spot, tokens:] = rows[here, tokens:].astype(jnp.bfloat16)
            at += 1


def pack(slots, width, experts, parts):
    blocks = sum(part.shape[0] for part in parts)
    shape = jax.ShapeDtypeStruct((2, blocks * slots, width), jnp.bfloat16)
    tokens = parts[0].shape[1]
    rows = len(SENT) * blocks * slots
    return pl.pallas_call(
        functools.partial(pack_kernel, slots),
        out_shape=[shape] * RING,
        in_specs=[pl.BlockSpec(memory_space=pltpu.VMEM)] * (1 + len(parts)),
        out_specs=[pl.BlockSpec(memory_space=pltpu.VMEM)] * RING,
        compiler_params=pltpu.CompilerParams(vmem_limit_bytes=18 << 20),
        cost_estimate=pl.CostEstimate(
            flops=2 * rows * tokens * width,
            transcendentals=0,
            bytes_accessed=2 * rows * width + 2 * blocks * tokens * width,
        ),
        name="pack_rows",
    )(experts, *parts)


def consume_kernel(which, more, *refs):
    rows, (wg, wu), refs = refs[:RING], refs[RING : RING + 2], refs[RING + 2 :]
    if more:
        before_ref, refs = refs[0], refs[1:]
    sum_ref, sem, x, h = refs
    n = rows[0].shape[1]
    ff = h.shape[1]
    copies = [
        pltpu.make_async_copy(rows[j].at[which], x.at[pl.ds(j * n, n)], sem.at[j])
        for j in range(RING)
    ]
    for copy in copies:
        copy.start()
    count = before_ref[ff:, :1] if more else jnp.zeros((EXTRA, 1), jnp.float32)
    group = RING if n < 128 else 2
    for j in range(0, RING, group):
        for copy in copies[j : j + group]:
            copy.wait()
        tile = x[pl.ds(j * n, group * n), :]
        gate = jnp.dot(tile, wg[0], preferred_element_type=jnp.float32)
        upward = jnp.dot(tile, wu[0], preferred_element_type=jnp.float32)
        live = tile[:, :1].astype(jnp.float32) < LIMIT
        hidden = gate / (1.0 + jnp.exp(-gate)) * upward
        h[pl.ds(j * n, group * n), :] = jnp.where(live, hidden, 0.0).astype(jnp.bfloat16)
        count += jnp.sum(live.astype(jnp.float32), axis=0, keepdims=True)
    gram = lax.dot_general(
        h[...], h[...], (((0,), (0,)), ((), ())), preferred_element_type=jnp.float32
    )
    sum_ref[:ff, :] = gram + before_ref[:ff, :] if more else gram
    sum_ref[ff:, :] = jnp.broadcast_to(count, (EXTRA, ff))


def consume(which, rows, w_gate, w_up, before=None):
    _, n, width = rows[0].shape
    ff = w_gate.shape[2]
    total = n * RING
    more = before is not None
    hbm, vmem = pl.BlockSpec(memory_space=pl.ANY), pl.BlockSpec(memory_space=pltpu.VMEM)
    operands = [*rows, w_gate, w_up]
    specs = [hbm] * RING + [vmem] * 2
    if more:
        operands.append(before)
        specs.append(vmem)
    return pl.pallas_call(
        functools.partial(consume_kernel, which, more),
        out_shape=jax.ShapeDtypeStruct((ff + EXTRA, ff), jnp.float32),
        in_specs=specs,
        out_specs=vmem,
        scratch_shapes=[
            pltpu.SemaphoreType.DMA((RING,)),
            pltpu.VMEM((total, width), jnp.bfloat16),
            pltpu.VMEM((total, ff), jnp.bfloat16),
        ],
        compiler_params=pltpu.CompilerParams(vmem_limit_bytes=18 << 20),
        cost_estimate=pl.CostEstimate(
            flops=4 * total * width * ff + 2 * total * ff * ff,
            transcendentals=total * ff,
            bytes_accessed=2 * total * width + 4 * width * ff + 8 * ff * ff,
        ),
        name="hidden_gram",
    )(*operands)


def finish_kernel(one_ref, two_ref, down_ref, out_ref, mean_ref):
    ff = mean_ref.shape[0]

    @pl.when(pl.program_id(0) == 0)
    def _():
        count = one_ref[ff : ff + 1, :1] + two_ref[ff : ff + 1, :1]
        mean = (one_ref[:ff, :] + two_ref[:ff, :]) / count
        mean_ref[...] = mean.astype(jnp.bfloat16)

    down = down_ref[0].astype(jnp.bfloat16)
    out_ref[0] = jnp.dot(mean_ref[...], down, preferred_element_type=jnp.float32)


def finish(one, two, down):
    _, ff, wide = down.shape
    part = pl.BlockSpec((1, ff, COLS), lambda i: (0, 0, i))
    whole = pl.BlockSpec(one.shape, lambda i: (0, 0))
    return pl.pallas_call(
        finish_kernel,
        out_shape=jax.ShapeDtypeStruct(down.shape, jnp.float32),
        grid=(wide // COLS,),
        in_specs=[whole, whole, part],
        out_specs=part,
        scratch_shapes=[pltpu.VMEM((ff, ff), jnp.bfloat16)],
        compiler_params=pltpu.CompilerParams(vmem_limit_bytes=18 << 20),
        name="mean_product",
    )(one, two, down)


def exchange(packed):
    sent = [move(packed[shift], owner_ring(shift), "F") for shift in (2, 1, 3)]
    return [packed[0], *sent]


def local(tokens, expert_ids, w_gate, w_up, down_error):
    experts = lax.axis_size("gx") * lax.axis_size("gy")
    count, top = expert_ids.shape
    width = tokens.shape[1]
    slots = 3 * count * top // experts
    me = lax.axis_index(AXES)
    targets = lax.dynamic_slice(jnp.asarray(TARGETS), (me, 0), (1, len(SENT)))
    targets = jnp.broadcast_to(targets[0][:, None], (len(SENT), count))
    ids = jnp.pad(expert_ids.T.astype(jnp.bfloat16), ((0, count - top), (0, 0)))
    own = jnp.concatenate([tokens, ids], axis=1)[None]

    def packed(*parts):
        return pack(slots, width, targets, parts)

    ring = [move(own, gather_ring(shift), "ring") for shift in (2, 1, -1)]
    own_up, own_down = move(own, along_y(1), "own"), move(own, along_y(-1), "own")
    ring = tie(*ring)
    near = jnp.concatenate(ring, axis=0)
    near, own = tie(near, own)
    near_up, near_down = move(near, along_y(1), "near"), move(near, along_y(-1), "near")
    rows_a = exchange(packed(own, *ring, own_up, own_down))
    mine = consume(0, rows_a, w_gate, w_up)
    near_up, near_down, mine, other_gate, other_up, *rows_a = tie(
        near_up, near_down, mine, w_gate, w_up, *rows_a
    )
    other_gate, other_up = move(other_gate, OTHER_CORE, "og"), move(other_up, OTHER_CORE, "ou")
    next_up = jnp.concatenate([own_up, near_up[:1]], axis=0)
    far_up, far_down = move(next_up, along_y(1), "far"), move(near_down[1:], along_y(-1), "far")
    rows_b = exchange(packed(near_up, near_down))
    theirs = consume(1, rows_a, other_gate, other_up)
    far_up, far_down, theirs, *rows_b = tie(far_up, far_down, theirs, *rows_b)
    rows_c = exchange(packed(far_up, far_down))
    mine = consume(0, rows_b, w_gate, w_up, mine)
    theirs = consume(1, rows_b, other_gate, other_up, theirs)
    mine, theirs, *rows_c = tie(mine, theirs, *rows_c)
    theirs = move(consume(1, rows_c, other_gate, other_up, theirs), OTHER_CORE, "sums")
    mine = consume(0, rows_c, w_gate, w_up, mine)
    return finish(mine, theirs, down_error)


def solution(mesh):
    return jax.shard_map(
        local,
        mesh=mesh,
        in_specs=(
            P(AXES, None),
            P(AXES, None),
            P(AXES, None, None),
            P(AXES, None, None),
            P(AXES, None, None),
        ),
        out_specs=P(AXES, None, None),
        check_vma=False,
    )
```

```python
import functools
import itertools

import jax
import jax.numpy as jnp
import numpy as np
from jax import lax
from jax.experimental import pallas as pl
from jax.experimental.pallas import tpu as pltpu
from jax.sharding import PartitionSpec as P

AXES = ("gx", "gy")
FREE = 64.0
LIMIT = 32.0
RING = 4
EXTRA = 8
SENT = [(shift, cross) for shift in range(RING) for cross in range(2)]
COLS = 512


def place(x, y, c, z):
    return ((x % RING * RING + y % RING) * 2 + c) * RING + z % RING


SPOTS = list(itertools.product(range(RING), range(RING), range(2), range(RING)))


def owner(shift, cross, x, y, c, z):
    return place(x + shift, y, c ^ cross, z) if c else place(x, y, c ^ cross, z + shift)


TARGETS = np.array([[owner(*sent, *spot) for sent in SENT] for spot in SPOTS], np.int32)


def along_y(shift):
    return [(place(x, y, c, z), place(x, y + shift, c, z)) for x, y, c, z in SPOTS]


def gather_ring(shift):
    return [
        (place(x, y, c, z), place(x, y, c, z + shift) if c else place(x + shift, y, c, z))
        for x, y, c, z in SPOTS
    ]


def owner_ring(shift):
    return [(place(*spot), owner(shift, 0, *spot)) for spot in SPOTS]


OTHER_CORE = [(place(x, y, c, z), place(x, y, 1 - c, z)) for x, y, c, z in SPOTS]


def move(value, route, name="y"):
    with jax.named_scope(name):
        return lax.ppermute(value, AXES, route)


def tie(*values):
    return lax.optimization_barrier(values)


def pack_kernel(slots, experts_ref, *refs):
    ins, outs = refs[:-RING], refs[-RING:]
    tokens = ins[0].shape[1]
    width = outs[0].shape[2]
    group = len(SENT)
    top = experts_ref.shape[0]
    experts = experts_ref[...].astype(jnp.float32)
    before = (
        lax.broadcasted_iota(jnp.int32, (tokens, tokens), 0)
        < lax.broadcasted_iota(jnp.int32, (tokens, tokens), 1)
    ).astype(jnp.bfloat16)
    slot = lax.broadcasted_iota(jnp.int32, (group, slots, tokens), 1).astype(jnp.float32)
    lane = lax.broadcasted_iota(jnp.int32, (group, slots, tokens), 2)
    at = 0
    for ref in ins:
        for b in range(ref.shape[0]):
            ids = ref[b, :top, width:].astype(jnp.float32)
            member = jnp.zeros((group, tokens), jnp.float32)
            for k in range(top):
                member += (ids[k : k + 1, :] == experts).astype(jnp.float32)
            rank = jnp.dot(member.astype(jnp.bfloat16), before, preferred_element_type=jnp.float32)
            rank = jnp.where(member > 0.5, rank, -1.0)
            total = jnp.sum(member, axis=1, keepdims=True)
            picks = (rank[:, None, :] == slot).astype(jnp.float32)
            picks = picks.reshape(group * slots, tokens).astype(jnp.bfloat16)
            rows = jnp.dot(picks, ref[b, :, :width], preferred_element_type=jnp.float32)
            free = (slot >= total[:, :, None]) & (lane == 0)
            mark = jnp.where(free, FREE, 0.0).reshape(group * slots, tokens)
            for g, (shift, cross) in enumerate(SENT):
                here = slice(g * slots, (g + 1) * slots)
                spot = slice(at * slots, (at + 1) * slots)
                out = outs[shift]
                out[cross, spot, :tokens] = (rows[here, :tokens] + mark[here]).astype(jnp.bfloat16)
                out[cross, spot, tokens:] = rows[here, tokens:].astype(jnp.bfloat16)
            at += 1


def pack(slots, width, experts, parts):
    blocks = sum(part.shape[0] for part in parts)
    shape = jax.ShapeDtypeStruct((2, blocks * slots, width), jnp.bfloat16)
    tokens = parts[0].shape[1]
    rows = len(SENT) * blocks * slots
    return pl.pallas_call(
        functools.partial(pack_kernel, slots),
        out_shape=[shape] * RING,
        in_specs=[pl.BlockSpec(memory_space=pltpu.VMEM)] * (1 + len(parts)),
        out_specs=[pl.BlockSpec(memory_space=pltpu.VMEM)] * RING,
        compiler_params=pltpu.CompilerParams(vmem_limit_bytes=18 << 20),
        cost_estimate=pl.CostEstimate(
            flops=2 * rows * tokens * width,
            transcendentals=0,
            bytes_accessed=2 * rows * width + 2 * blocks * tokens * width,
        ),
        name="pack_rows",
    )(experts, *parts)


def consume_kernel(which, more, parts, *refs):
    rows, (wg, wu), refs = refs[:parts], refs[parts : parts + 2], refs[parts + 2 :]
    if more:
        before_ref, refs = refs[0], refs[1:]
    sum_ref, sem, x, h = refs
    n = rows[0].shape[1]
    ff = h.shape[1]
    copies = [
        pltpu.make_async_copy(rows[j].at[which], x.at[pl.ds(j * n, n)], sem.at[j])
        for j in range(parts)
    ]
    for copy in copies:
        copy.start()
    count = before_ref[ff:, :1] if more else jnp.zeros((EXTRA, 1), jnp.float32)
    group = parts if n < 128 else 2
    for j in range(0, parts, group):
        for copy in copies[j : j + group]:
            copy.wait()
        tile = x[pl.ds(j * n, group * n), :]
        gate = jnp.dot(tile, wg[0], preferred_element_type=jnp.float32)
        upward = jnp.dot(tile, wu[0], preferred_element_type=jnp.float32)
        live = tile[:, :1].astype(jnp.float32) < LIMIT
        hidden = gate / (1.0 + jnp.exp(-gate)) * upward
        h[pl.ds(j * n, group * n), :] = jnp.where(live, hidden, 0.0).astype(jnp.bfloat16)
        count += jnp.sum(live.astype(jnp.float32), axis=0, keepdims=True)
    gram = lax.dot_general(
        h[...], h[...], (((0,), (0,)), ((), ())), preferred_element_type=jnp.float32
    )
    sum_ref[:ff, :] = gram + before_ref[:ff, :] if more else gram
    sum_ref[ff:, :] = jnp.broadcast_to(count, (EXTRA, ff))


def consume(which, rows, w_gate, w_up, before=None):
    _, n, width = rows[0].shape
    parts = len(rows)
    ff = w_gate.shape[2]
    total = n * parts
    more = before is not None
    hbm, vmem = pl.BlockSpec(memory_space=pl.ANY), pl.BlockSpec(memory_space=pltpu.VMEM)
    operands = [*rows, w_gate, w_up]
    specs = [hbm] * parts + [vmem] * 2
    if more:
        operands.append(before)
        specs.append(vmem)
    return pl.pallas_call(
        functools.partial(consume_kernel, which, more, parts),
        out_shape=jax.ShapeDtypeStruct((ff + EXTRA, ff), jnp.float32),
        in_specs=specs,
        out_specs=vmem,
        scratch_shapes=[
            pltpu.SemaphoreType.DMA((parts,)),
            pltpu.VMEM((total, width), jnp.bfloat16),
            pltpu.VMEM((total, ff), jnp.bfloat16),
        ],
        compiler_params=pltpu.CompilerParams(vmem_limit_bytes=18 << 20),
        cost_estimate=pl.CostEstimate(
            flops=4 * total * width * ff + 2 * total * ff * ff,
            transcendentals=total * ff,
            bytes_accessed=2 * total * width + 4 * width * ff + 8 * ff * ff,
        ),
        name="hidden_gram",
    )(*operands)


def finish_kernel(one_ref, two_ref, down_ref, out_ref, mean_ref):
    ff = mean_ref.shape[0]

    @pl.when(pl.program_id(0) == 0)
    def _():
        count = one_ref[ff : ff + 1, :1] + two_ref[ff : ff + 1, :1]
        mean = (one_ref[:ff, :] + two_ref[:ff, :]) / count
        mean_ref[...] = mean.astype(jnp.bfloat16)

    down = down_ref[0].astype(jnp.bfloat16)
    out_ref[0] = jnp.dot(mean_ref[...], down, preferred_element_type=jnp.float32)


def finish(one, two, down):
    _, ff, wide = down.shape
    part = pl.BlockSpec((1, ff, COLS), lambda i: (0, 0, i))
    whole = pl.BlockSpec(one.shape, lambda i: (0, 0))
    return pl.pallas_call(
        finish_kernel,
        out_shape=jax.ShapeDtypeStruct(down.shape, jnp.float32),
        grid=(wide // COLS,),
        in_specs=[whole, whole, part],
        out_specs=part,
        scratch_shapes=[pltpu.VMEM((ff, ff), jnp.bfloat16)],
        compiler_params=pltpu.CompilerParams(vmem_limit_bytes=18 << 20),
        name="mean_product",
    )(one, two, down)


def exchange(packed):
    sent = [move(packed[shift], owner_ring(shift), "F") for shift in (2, 1, 3)]
    return [packed[0], *sent]


def local(tokens, expert_ids, w_gate, w_up, down_error):
    experts = lax.axis_size("gx") * lax.axis_size("gy")
    count, top = expert_ids.shape
    width = tokens.shape[1]
    slots = 3 * count * top // experts
    me = lax.axis_index(AXES)
    targets = lax.dynamic_slice(jnp.asarray(TARGETS), (me, 0), (1, len(SENT)))
    targets = jnp.broadcast_to(targets[0][:, None], (len(SENT), count))
    ids = jnp.pad(expert_ids.T.astype(jnp.bfloat16), ((0, count - top), (0, 0)))
    own = jnp.concatenate([tokens, ids], axis=1)[None]

    def packed(*parts):
        return pack(slots, width, targets, parts)

    ring = [move(own, gather_ring(shift), "ring") for shift in (2, 1, -1)]
    own_up, own_down = move(own, along_y(1), "own"), move(own, along_y(-1), "own")
    ring = tie(*ring)
    near = jnp.concatenate(ring, axis=0)
    near, own = tie(near, own)
    near_up, near_down = move(near, along_y(1), "near"), move(near, along_y(-1), "near")
    rows_a = exchange(packed(own, *ring, own_up, own_down))
    mine = consume(0, rows_a, w_gate, w_up)
    near_up, near_down, mine, other_gate, other_up, *rows_a = tie(
        near_up, near_down, mine, w_gate, w_up, *rows_a
    )
    other_gate, other_up = move(other_gate, OTHER_CORE, "og"), move(other_up, OTHER_CORE, "ou")
    next_up = jnp.concatenate([own_up, near_up[:1]], axis=0)
    far_up, far_down = move(next_up, along_y(1), "far"), move(near_down[1:], along_y(-1), "far")
    rows_b = exchange(packed(near_up, near_down))
    theirs = consume(1, rows_a, other_gate, other_up)
    far_up, far_down, theirs, *rows_b = tie(far_up, far_down, theirs, *rows_b)
    rows_c = exchange(packed(far_up, far_down))
    mine = consume(0, rows_b, w_gate, w_up, mine)
    theirs = consume(1, rows_b, other_gate, other_up, theirs)
    early, late = rows_c[:2], rows_c[2:]
    mine = consume(0, early, w_gate, w_up, mine)
    theirs = consume(1, early, other_gate, other_up, theirs)
    mine, theirs, *late = tie(mine, theirs, *late)
    theirs = move(consume(1, late, other_gate, other_up, theirs), OTHER_CORE, "sums")
    mine = consume(0, late, w_gate, w_up, mine)
    return finish(mine, theirs, down_error)


def solution(mesh):
    return jax.shard_map(
        local,
        mesh=mesh,
        in_specs=(
            P(AXES, None),
            P(AXES, None),
            P(AXES, None, None),
            P(AXES, None, None),
            P(AXES, None, None),
        ),
        out_specs=P(AXES, None, None),
        check_vma=False,
    )
```
